32 devices in a mesh: groups: 2 (over y), slab: 4 (over z), chan: 4 (over x, core).
Axes of the slice: x: 2, y: 2, z: 4, core: 2. Of those that a mesh axis runs over, the one named last changes fastest.
Arguments:
- field: float32 [64, 8, 512], P('chan', ('groups', 'slab')), parts along dimension 1, may hold values from -6 to 6
- order: int32 [2, 64], replicated, may hold values from 0 to 63, each once within a row
- w_first: bfloat16 [2, 512, 864], P(None, 'chan'), may hold values from -0.21875 to 0.21875
- b_first: bfloat16 [2, 512], P(None, 'chan'), may hold values from -3 to 3
- w_middle: bfloat16 [2, 512, 512], P(None, 'chan'), may hold values from -0.375 to 0.375
- b_middle: bfloat16 [2, 512], P(None, 'chan'), may hold values from -3 to 3
- w_last: bfloat16 [2, 1728, 512], P(None, None, 'chan'), may hold values from -0.078125 to 0.078125
- b_last: bfloat16 [2, 64], replicated, may hold values from -3 to 3
Outputs:
- flowed: float32 [64, 8, 512], P('chan', ('groups', 'slab')), parts along dimension 1
- logscale: float32 [2, 32, 8], P(None, 'chan', ('groups', 'slab')), parts along dimension 2
The draws below stay inside these ranges and needn't reach their ends.
There are 2 independent parts, one for each index of `groups`. The reference program is written for one: setup_inputs(seed, part) draws one part's arguments, and reference() takes and returns one part's arrays. A program takes and returns all parts, laid end to end along the dimension named above; an argument that names none is the same for every part. Nothing has to cross between parts.
Inputs may be any that keep to these rules, and one draw needn't show every extreme that they name: Each row of order names every channel once.
All inputs are finite; a program needn't handle non-finite values.
Results may differ from the reference program's by a relative error of at most 0.0095.
Values may be sent and summed in bfloat16 or wider, within the bound.
A program may use at most 64 MiB of HBM per device.

```python
import jax
import jax.numpy as jnp
from jax import lax

C = 64
HID = 512
STEPS = 2
NX = 8
NY = 64
NZ = 4
NXY = 512
HALF = 32
K1 = 864
K3 = 1728


def levels(stream_key, shape, shards, least, largest):
    factor_of = 1.0
    for position, blocks in shards:
        draws = jax.random.uniform(jax.random.fold_in(jax.random.fold_in(stream_key, 6), position), (blocks,), jnp.float32, least / len(shards), largest / len(shards))
        factor_of = factor_of * jnp.repeat(jnp.exp(draws), shape[position] // blocks).reshape((-1,) + (1,) * (len(shape) - 1 - position))
    return factor_of


def bell_draw(rng, dims, width, reach, pieces=(), dtype=jnp.bfloat16):
    values = width * jax.random.normal(rng, dims, jnp.float32)
    if pieces:
        values = values * levels(rng, dims, pieces, -0.22, 0.18)
    return jnp.clip(values, -reach, reach).astype(dtype)


def setup_inputs(seed: int = 0, part: int = 0) -> dict:
    key_list = jax.random.split(jax.random.key(seed), 9)
    part_keys = jax.random.split(jax.random.fold_in(key_list[8], part), 9)
    return {
        "field": bell_draw(part_keys[0], (C, NZ, NXY), 1.0, 6.0, ((0, 4), (1, 4)), jnp.float32),
        "order": jax.vmap(lambda own: jax.random.permutation(own, C))(jax.random.split(key_list[1], STEPS)).reshape((STEPS, C)).astype(jnp.int32),
        "w_first": bell_draw(key_list[2], (STEPS, HID, K1), K1 ** -0.5, 0.21875, ((1, 4),)),
        "b_first": bell_draw(key_list[3], (STEPS, HID), 0.5, 3.0, ((1, 4),)),
        "w_middle": bell_draw(key_list[4], (STEPS, HID, HID), (HID // 2) ** -0.5, 0.375, ((1, 4),)),
        "b_middle": bell_draw(key_list[5], (STEPS, HID), 0.5, 3.0, ((1, 4),)),
        "w_last": bell_draw(key_list[6], (STEPS, K3, HID), (HID * 27 // 2) ** -0.5, 0.078125, ((2, 4),)),
        "b_last": bell_draw(key_list[7], (STEPS, C), 0.5, 3.0),
    }


def conv_same(inputs, kernel):
    result = lax.conv_general_dilated(inputs[None], kernel, (1, 1, 1), ((1, 1), (1, 1), (1, 1)), dimension_numbers=("NCDHW", "OIDHW", "NCDHW"), precision=lax.Precision.HIGHEST)
    return result[0]


def reference(field, order, w_first, b_first, w_middle, b_middle, w_last, b_last):
    current = field
    records = []
    for section in range(STEPS):
        permuted = jnp.take(current, order[section], axis=0)
        front = permuted[:HALF]
        back = permuted[HALF:]
        front_bf = lax.optimization_barrier(front.astype(jnp.bfloat16))
        grid_in = front_bf.astype(jnp.float32).reshape(HALF, NZ, NX, NY)
        kernel_one = w_first[section].astype(jnp.float32).reshape(HID, 3, 3, 3, HALF).transpose(0, 4, 1, 2, 3)
        hidden_one = jax.nn.relu(conv_same(grid_in, kernel_one) + b_first[section].astype(jnp.float32)[:, None, None, None])
        hidden_one = hidden_one.astype(jnp.bfloat16).reshape(HID, NZ * NXY)
        middle = jnp.dot(w_middle[section], hidden_one, preferred_element_type=jnp.float32)
        hidden_two = jax.nn.relu(middle + b_middle[section].astype(jnp.float32)[:, None]).astype(jnp.bfloat16)
        kernel_three = w_last[section].astype(jnp.float32).reshape(3, 3, 3, C, HID).transpose(3, 4, 0, 1, 2)
        net = conv_same(hidden_two.astype(jnp.float32).reshape(HID, NZ, NX, NY), kernel_three)
        net = net.reshape(C, NZ, NXY) + b_last[section].astype(jnp.float32)[:, None, None]
        shifted = net[:HALF] + 2.0
        scale = jax.nn.sigmoid(shifted)
        coupled = (back + net[HALF:]) * scale
        records.append(jnp.mean(jax.nn.log_sigmoid(shifted), axis=2))
        current = jnp.concatenate([front, coupled], axis=0)
    return current, jnp.stack(records)
```

```python
import jax
import jax.numpy as jnp
from jax import lax
from jax.experimental import pallas as pl
from jax.experimental.pallas import tpu as pltpu
from jax.sharding import PartitionSpec as P

C = 64
HALF = 32
STEPS = 2
NY = 64
NXY = 512
PAD = 128
MESH = pl.DeviceIdType.MESH
F32 = jnp.float32
BF16 = jnp.bfloat16


def kernel(
    field, order, w_first, b_first, w_middle, b_middle, w_last, b_last,
    flowed, logscale,
    field_in, wf, wm, wl, bias1, bias2, bias3, perm,
    whole, xpad, patches, hidden, hpad, patches3, psend, precv,
    back, csend, cgot, fronts, final_send, final,
    load_sem, send_sem, recv_sem, out_sem,
):
    n_chan = lax.axis_size("chan")
    n_slab = lax.axis_size("slab")
    c = lax.axis_index("chan")
    z = lax.axis_index("slab")
    share = HALF // n_chan
    own = C // n_chan
    units = wf.shape[2]
    has = {0: z > 0, 1: None, 2: z < n_slab - 1}

    def peer(dz, j):
        return {"slab": z + dz, "chan": lax.rem(c + j, n_chan)}

    def each_peer(fn):
        @pl.when(z > 0)
        def _():
            for j in range(n_chan):
                fn(-1, j)

        @pl.when(z < n_slab - 1)
        def _():
            for j in range(n_chan):
                fn(1, j)

        for j in range(1, n_chan):
            fn(0, j)

    loads = [pltpu.make_async_copy(field.at[:, 0, :], field_in, load_sem.at[0])]
    loads.append(pltpu.make_async_copy(w_first, wf, load_sem.at[1]))
    loads.append(pltpu.make_async_copy(w_middle, wm, load_sem.at[2]))
    n = 3
    for k in range(STEPS):
        for a in range(3):
            loads.append(
                pltpu.make_async_copy(
                    w_last.at[k, a], wl.at[k, :, pl.ds(a * C, C), :], load_sem.at[n]
                )
            )
            n += 1
    for load in loads:
        load.start()

    barrier = pltpu.get_barrier_semaphore()

    def greet(dz, j):
        pl.semaphore_signal(barrier, inc=1, device_id=peer(dz, j), device_id_type=MESH)

    each_peer(greet)

    for k in range(STEPS):
        row = order[k : k + 1, :]
        hit = (lax.broadcasted_iota(jnp.int32, (C, C), 0) == row).astype(F32)
        perm[k] = hit.T.astype(BF16)
        bias1[k] = jnp.broadcast_to(b_first[k : k + 1, :].astype(F32), (128, units)).T
        bias2[k] = jnp.broadcast_to(b_middle[k : k + 1, :].astype(F32), (128, units)).T
        bias3[k] = jnp.broadcast_to(b_last[k : k + 1, :].astype(F32), (128, C)).T
    for e in range(3):
        xpad[e, :, 0:PAD] = jnp.zeros((3 * HALF, PAD), BF16)
        xpad[e, :, PAD + NXY :] = jnp.zeros((3 * HALF, PAD), BF16)
        hpad[e, :, 0:PAD] = jnp.zeros((units, PAD), BF16)
        hpad[e, :, PAD + NXY :] = jnp.zeros((units, PAD), BF16)
    for a in (0, 2):

        @pl.when(jnp.logical_not(has[a]))
        def _():
            whole[a] = jnp.zeros((C, NXY), BF16)
            cgot[a] = jnp.zeros((n_chan, 2 * share, NXY // 2), BF16)
            for k in range(STEPS):
                precv[k, a] = jnp.zeros((n_chan, 2 * share, NXY), BF16)

    mine = pl.ds(pl.multiple_of(c * own, own), own)
    loads[0].wait()
    whole[1, mine, :] = field_in[...].astype(BF16)

    sides = jnp.where(z > 0, 1, 0) + jnp.where(z < n_slab - 1, 1, 0)
    pl.semaphore_wait(barrier, n_chan - 1 + n_chan * sides)

    def copy(phase, dz, j, src, dst):
        return pltpu.make_async_remote_copy(
            src_ref=src,
            dst_ref=dst,
            send_sem=send_sem.at[phase, 1 - dz, j],
            recv_sem=recv_sem.at[phase, 1 - dz, j],
            device_id=peer(dz, j),
            device_id_type=MESH,
        )

    def arrive(phase, a, j, dst):
        pltpu.make_async_remote_copy(
            src_ref=dst,
            dst_ref=dst,
            send_sem=send_sem.at[phase, a, j],
            recv_sem=recv_sem.at[phase, a, j],
            device_id=peer(0, 1),
            device_id_type=MESH,
        ).wait_recv()

    def each_source(fn):
        for j in range(1, n_chan):
            fn(1, j)

        @pl.when(z > 0)
        def _():
            for j in range(n_chan):
                fn(0, j)

        @pl.when(z < n_slab - 1)
        def _():
            for j in range(n_chan):
                fn(2, j)

    def source(j):
        return lax.rem(c + n_chan - j, n_chan)

    def send_field(dz, j):
        copy(0, dz, j, whole.at[1, mine, :], whole.at[1 - dz, mine, :]).start()

    each_peer(send_field)

    def field_arrives(a, j):
        rows = pl.ds(pl.multiple_of(source(j) * own, own), own)
        arrive(0, a, j, whole.at[a, rows, :])

    each_source(field_arrives)

    y = lax.rem(lax.broadcasted_iota(jnp.int32, (1, NXY), 1), NY)

    def keep(values, e):
        if e == 0:
            return jnp.where(y == NY - 1, 0.0, values)
        if e == 2:
            return jnp.where(y == 0, 0.0, values)
        return values

    def shifted(b, e):
        start = PAD + NY * (b - 1) + (e - 1)
        return slice(start, start + NXY)

    def wide(column):
        return jnp.concatenate([column] * (NXY // 128), axis=1)

    for k in range(STEPS):
        for a in range(3):
            if k == 0:
                plane = whole[a]
            else:
                got = [cgot[a, s].astype(F32) for s in range(n_chan)]
                got = [jnp.concatenate([g[:share], g[share:]], axis=1) for g in got]
                plane = jnp.concatenate([fronts[a]] + got, axis=0).astype(BF16)
            if a == 1:
                permuted = jnp.dot(perm[k], plane, preferred_element_type=F32)
                back[...] = permuted
                front = permuted[:HALF]
            else:
                front = jnp.dot(perm[k, 0:HALF, :], plane, preferred_element_type=F32)
            if k == 0:
                fronts[a] = front
            for e in range(3):
                xpad[e, a * HALF : (a + 1) * HALF, PAD : PAD + NXY] = keep(front, e).astype(BF16)
        for a in range(3):
            for b in range(3):
                for e in range(3):
                    at = ((a * 3 + b) * 3 + e) * HALF
                    patches[at : at + HALF, :] = xpad[e, a * HALF : (a + 1) * HALF, shifted(b, e)]
        if k == 0:
            loads[1].wait()
        total = lax.dot_general(
            wf[k], patches[...], (((0,), (0,)), ((), ())), preferred_element_type=F32
        )
        rows = pl.ds(pl.multiple_of(c * units, units), units)
        hidden[k, rows, :] = jnp.maximum(total + wide(bias1[k]), 0.0).astype(BF16)
        for j in range(1, n_chan):
            copy(1 + k, 0, j, hidden.at[k, rows, :], hidden.at[k, rows, :]).start()
        if k == 0:
            for load in loads[2:]:
                load.wait()
        summed = jnp.dot(wm[k, :, rows], hidden[k, rows, :], preferred_element_type=F32)
        for j in range(1, n_chan):
            theirs = pl.ds(pl.multiple_of(source(j) * units, units), units)
            arrive(1 + k, 1, j, hidden.at[k, theirs, :])
            summed += jnp.dot(wm[k, :, theirs], hidden[k, theirs, :], preferred_element_type=F32)
        two = jnp.maximum(summed + wide(bias2[k]), 0.0)
        for e in range(3):
            hpad[e, :, PAD : PAD + NXY] = keep(two, e).astype(BF16)
        for b in range(3):
            for e in range(3):
                at = (b * 3 + e) * units
                patches3[at : at + units, :] = hpad[e, :, shifted(b, e)]
        weights = jnp.concatenate([wl[k, i] for i in range(9)], axis=1)
        parts = jnp.dot(weights, patches3[...], preferred_element_type=F32)
        for s in range(n_chan):
            for a in range(3):
                low = a * C + s * share
                psend[k, s, a] = jnp.concatenate(
                    [parts[low : low + share], parts[low + HALF : low + HALF + share]], axis=0
                ).astype(BF16)

        def send_parts(dz, j):
            to = lax.rem(c + j, n_chan)
            copy(3 + k, dz, j, psend.at[k, to, 1 - dz], precv.at[k, 1 - dz, c]).start()

        each_peer(send_parts)
        precv[k, 1, c] = psend[k, c, 1]

        def parts_arrive(a, j):
            arrive(3 + k, a, j, precv.at[k, a, source(j)])

        each_source(parts_arrive)
        net = precv[k, 1, 0].astype(F32)
        for a in range(3):
            for s in range(n_chan):
                if (a, s) != (1, 0):
                    net = net + precv[k, a, s].astype(F32)
        scales = pl.ds(pl.multiple_of(c * share, share), share)
        shifts = pl.ds(pl.multiple_of(HALF + c * share, share), share)
        arg = net[:share] + wide(bias3[k, scales, :]) + 2.0
        coupled = (back[shifts, :] + net[share:] + wide(bias3[k, shifts, :])) * jax.nn.sigmoid(arg)
        if k == 0:
            packed = jnp.concatenate([coupled[:, : NXY // 2], coupled[:, NXY // 2 :]], axis=0)
            csend[...] = packed.astype(BF16)

            def send_coupled(dz, j):
                copy(5, dz, j, csend, cgot.at[1 - dz, c]).start()

            each_peer(send_coupled)
            cgot[1, c] = packed.astype(BF16)
        else:
            final_send[...] = coupled
            keeper = n_chan // 2 + c // 2
            place = pl.ds(pl.multiple_of(lax.rem(c, 2) * share, share), share)
            last = pltpu.make_async_remote_copy(
                src_ref=final_send,
                dst_ref=final.at[place, :],
                send_sem=send_sem.at[6, 1, 0],
                recv_sem=recv_sem.at[6, 1, lax.rem(c, 2)],
                device_id={"chan": keeper},
                device_id_type=MESH,
            )

            @pl.when(keeper != c)
            def _():
                last.start()

            @pl.when(keeper == c)
            def _():
                final[place, :] = coupled

        soft = jnp.minimum(arg, 0.0) - jnp.log1p(jnp.exp(-jnp.abs(arg)))
        means = jnp.broadcast_to(jnp.sum(soft, axis=1, keepdims=True) * (1.0 / NXY), (share, share))
        diagonal = lax.broadcasted_iota(jnp.int32, (share, share), 0) == lax.broadcasted_iota(
            jnp.int32, (share, share), 1
        )
        logscale[k] = jnp.sum(jnp.where(diagonal, means, 0.0), axis=0, keepdims=True)
        if k == 0:

            def coupled_arrives(a, j):
                arrive(5, a, j, cgot.at[a, source(j)])

            each_source(coupled_arrives)

    for i in range(2):
        sender = 2 * (c - n_chan // 2) + i
        place = slice(i * share, (i + 1) * share)

        @pl.when(jnp.logical_and(c >= n_chan // 2, sender != c))
        def _():
            pltpu.make_async_remote_copy(
                src_ref=final_send,
                dst_ref=final.at[place, :],
                send_sem=send_sem.at[6, 1, 0],
                recv_sem=recv_sem.at[6, 1, i],
                device_id=peer(0, 1),
                device_id_type=MESH,
            ).wait_recv()

    @pl.when(c < n_chan // 2)
    def _():
        at = pl.ds(pl.multiple_of(lax.rem(c, 2) * own, own), own)
        final[...] = back[at, :]

    out = pltpu.make_async_copy(final, flowed.at[:, 0, :], out_sem)
    out.start()

    each_peer(lambda dz, j: copy(0, dz, j, whole.at[1, mine, :], whole.at[1 - dz, mine, :]).wait_send())
    for k in range(STEPS):
        rows = pl.ds(pl.multiple_of(c * units, units), units)
        for j in range(1, n_chan):
            copy(1 + k, 0, j, hidden.at[k, rows, :], hidden.at[k, rows, :]).wait_send()
        each_peer(
            lambda dz, j: copy(
                3 + k, dz, j, psend.at[k, lax.rem(c + j, n_chan), 1 - dz], precv.at[k, 1 - dz, c]
            ).wait_send()
        )
    each_peer(lambda dz, j: copy(5, dz, j, csend, cgot.at[1 - dz, c]).wait_send())

    @pl.when(n_chan // 2 + c // 2 != c)
    def _():
        last.wait_send()

    out.wait()


def local(field, order, w_first, b_first, w_middle, b_middle, w_last, b_last):
    n_chan = lax.axis_size("chan")
    share = HALF // n_chan
    own = C // n_chan
    units = w_first.shape[1]
    vmem = pl.BlockSpec(memory_space=pltpu.VMEM)
    hbm = pl.BlockSpec(memory_space=pl.ANY)
    flowed, logscale = pl.pallas_call(
        kernel,
        out_shape=(
            jax.ShapeDtypeStruct(field.shape, F32),
            jax.ShapeDtypeStruct((STEPS, 1, share), F32),
        ),
        in_specs=[hbm, vmem, hbm, vmem, hbm, vmem, hbm, vmem],
        out_specs=(hbm, vmem),
        scratch_shapes=[
            pltpu.VMEM((own, NXY), F32),
            pltpu.VMEM((STEPS, 27 * HALF, units), BF16),
            pltpu.VMEM(w_middle.shape, BF16),
            pltpu.VMEM((STEPS, 9, 3 * C, units), BF16),
            pltpu.VMEM((STEPS, units, 128), F32),
            pltpu.VMEM((STEPS, units, 128), F32),
            pltpu.VMEM((STEPS, C, 128), F32),
            pltpu.VMEM((STEPS, C, C), BF16),
            pltpu.VMEM((3, C, NXY), BF16),
            pltpu.VMEM((3, 3 * HALF, NXY + 2 * PAD), BF16),
            pltpu.VMEM((27 * HALF, NXY), BF16),
            pltpu.VMEM((STEPS, n_chan * units, NXY), BF16),
            pltpu.VMEM((3, units, NXY + 2 * PAD), BF16),
            pltpu.VMEM((9 * units, NXY), BF16),
            pltpu.VMEM((STEPS, n_chan, 3, 2 * share, NXY), BF16),
            pltpu.VMEM((STEPS, 3, n_chan, 2 * share, NXY), BF16),
            pltpu.VMEM((C, NXY), F32),
            pltpu.VMEM((2 * share, NXY // 2), BF16),
            pltpu.VMEM((3, n_chan, 2 * share, NXY // 2), BF16),
            pltpu.VMEM((3, HALF, NXY), F32),
            pltpu.VMEM((share, NXY), F32),
            pltpu.VMEM((own, NXY), F32),
            pltpu.SemaphoreType.DMA((9,)),
            pltpu.SemaphoreType.DMA((7, 3, n_chan)),
            pltpu.SemaphoreType.DMA((7, 3, n_chan)),
            pltpu.SemaphoreType.DMA,
        ],
        compiler_params=pltpu.CompilerParams(
            collective_id=0, has_side_effects=True, vmem_limit_bytes=48 << 20
        ),
    )(
        field, order, jnp.swapaxes(w_first, 1, 2), b_first, w_middle, b_middle,
        w_last.reshape(STEPS, 3, 9, C, units), b_last,
    )
    return flowed, jnp.swapaxes(logscale, 1, 2)


def solution(mesh):
    return jax.shard_map(
        local,
        mesh=mesh,
        in_specs=(
            P("chan", ("groups", "slab"), None),
            P(),
            P(None, "chan", None),
            P(None, "chan"),
            P(None, "chan", None),
            P(None, "chan"),
            P(None, None, "chan"),
            P(),
        ),
        out_specs=(P("chan", ("groups", "slab"), None), P(None, "chan", ("groups", "slab"))),
        check_vma=False,
    )
```

```python
import jax
import jax.numpy as jnp
from jax import lax
from jax.experimental import pallas as pl
from jax.experimental.pallas import tpu as pltpu
from jax.sharding import PartitionSpec as P

C = 64
HALF = 32
STEPS = 2
NY = 64
NXY = 512
PAD = 128
MESH = pl.DeviceIdType.MESH
F32 = jnp.float32
BF16 = jnp.bfloat16


def kernel(
    field, order, w_first, b_first, w_middle, b_middle, w_last, b_last,
    flowed, logscale,
    field_in, wf, wm, wl, bias1, bias2, bias3, perm,
    whole, xpad, patches, hidden, hpad, patches3, psend, precv,
    back, csend, cgot, fronts, final_send, final,
    load_sem, send_sem, recv_sem, out_sem,
):
    n_chan = lax.axis_size("chan")
    assert n_chan == 4
    n_slab = lax.axis_size("slab")
    c = lax.axis_index("chan")
    z = lax.axis_index("slab")
    share = HALF // n_chan
    own = C // n_chan
    units = wf.shape[2]
    has = {0: z > 0, 1: None, 2: z < n_slab - 1}

    place_of = (c, c + 1 - 2 * lax.rem(c, 2), lax.rem(c + 2, 4), 3 - c)

    def peer(dz, j):
        return {"slab": z + dz, "chan": place_of[j]}

    def each_peer(fn):
        for j in (2, 3, 1):
            fn(0, j)

        @pl.when(z > 0)
        def _():
            for j in range(n_chan):
                fn(-1, j)

        @pl.when(z < n_slab - 1)
        def _():
            for j in range(n_chan):
                fn(1, j)

    loads = [pltpu.make_async_copy(field.at[:, 0, :], field_in, load_sem.at[0])]
    loads.append(pltpu.make_async_copy(w_first, wf, load_sem.at[1]))
    loads.append(pltpu.make_async_copy(w_middle, wm, load_sem.at[2]))
    n = 3
    for k in range(STEPS):
        for a in range(3):
            loads.append(
                pltpu.make_async_copy(
                    w_last.at[k, a], wl.at[k, :, pl.ds(a * C, C), :], load_sem.at[n]
                )
            )
            n += 1
    for load in loads:
        load.start()

    barrier = pltpu.get_barrier_semaphore()

    def greet(dz, j):
        pl.semaphore_signal(barrier, inc=1, device_id=peer(dz, j), device_id_type=MESH)

    each_peer(greet)

    for k in range(STEPS):
        row = order[k : k + 1, :]
        hit = (lax.broadcasted_iota(jnp.int32, (C, C), 0) == row).astype(F32)
        perm[k] = hit.T.astype(BF16)
        bias1[k] = jnp.broadcast_to(b_first[k : k + 1, :].astype(F32), (128, units)).T
        bias2[k] = jnp.broadcast_to(b_middle[k : k + 1, :].astype(F32), (128, units)).T
        bias3[k] = jnp.broadcast_to(b_last[k : k + 1, :].astype(F32), (128, C)).T
    for e in range(3):
        xpad[e, :, 0:PAD] = jnp.zeros((3 * HALF, PAD), BF16)
        xpad[e, :, PAD + NXY :] = jnp.zeros((3 * HALF, PAD), BF16)
        hpad[e, :, 0:PAD] = jnp.zeros((units, PAD), BF16)
        hpad[e, :, PAD + NXY :] = jnp.zeros((units, PAD), BF16)
    for a in (0, 2):

        @pl.when(jnp.logical_not(has[a]))
        def _():
            whole[a] = jnp.zeros((C, NXY), BF16)
            cgot[a] = jnp.zeros((n_chan, 2 * share, NXY // 2), BF16)
            for k in range(STEPS):
                precv[k, a] = jnp.zeros((n_chan, 2 * share, NXY), BF16)

    mine = pl.ds(pl.multiple_of(c * own, own), own)
    loads[0].wait()
    whole[1, mine, :] = field_in[...].astype(BF16)

    sides = jnp.where(z > 0, 1, 0) + jnp.where(z < n_slab - 1, 1, 0)
    pl.semaphore_wait(barrier, n_chan - 1 + n_chan * sides)

    def copy(phase, dz, j, src, dst):
        return pltpu.make_async_remote_copy(
            src_ref=src,
            dst_ref=dst,
            send_sem=send_sem.at[phase, 1 - dz, j],
            recv_sem=recv_sem.at[phase, 1 - dz, j],
            device_id=peer(dz, j),
            device_id_type=MESH,
        )

    def arrive(phase, a, j, dst):
        pltpu.make_async_remote_copy(
            src_ref=dst,
            dst_ref=dst,
            send_sem=send_sem.at[phase, a, j],
            recv_sem=recv_sem.at[phase, a, j],
            device_id=peer(0, 1),
            device_id_type=MESH,
        ).wait_recv()

    def centre_sources(fn):
        for j in (1, 2, 3):
            fn(1, j)

    def side_sources(fn):
        @pl.when(z > 0)
        def _():
            for j in range(n_chan):
                fn(0, j)

        @pl.when(z < n_slab - 1)
        def _():
            for j in range(n_chan):
                fn(2, j)

    def source(j):
        return place_of[j]

    def send_field(dz, j):
        copy(0, dz, j, whole.at[1, mine, :], whole.at[1 - dz, mine, :]).start()

    each_peer(send_field)

    def field_arrives(a, j):
        rows = pl.ds(pl.multiple_of(source(j) * own, own), own)
        arrive(0, a, j, whole.at[a, rows, :])

    y = lax.rem(lax.broadcasted_iota(jnp.int32, (1, NXY), 1), NY)

    def keep(values, e):
        if e == 0:
            return jnp.where(y == NY - 1, 0.0, values)
        if e == 2:
            return jnp.where(y == 0, 0.0, values)
        return values

    def shifted(b, e):
        start = PAD + NY * (b - 1) + (e - 1)
        return slice(start, start + NXY)

    def wide(column):
        return jnp.concatenate([column] * (NXY // 128), axis=1)

    def coupled_arrives(a, j):
        arrive(5, a, j, cgot.at[a, source(j)])

    half = NXY // 2

    def convolve(k, a, q):
        depth = slice(a * 9 * HALF, (a + 1) * 9 * HALF)
        return lax.dot_general(
            wf[k, depth, :],
            patches[depth, q * half : (q + 1) * half],
            (((0,), (0,)), ((), ())),
            preferred_element_type=F32,
        )

    def hidden_copy(k, q, j, owner):
        part = hidden.at[k, q, pl.ds(pl.multiple_of(owner * units, units), units), :]
        return pltpu.make_async_remote_copy(
            src_ref=part,
            dst_ref=part,
            send_sem=send_sem.at[1 + k, q, j],
            recv_sem=recv_sem.at[1 + k, q, j],
            device_id=peer(0, 1 if j == 3 else j),
            device_id_type=MESH,
        )

    for k in range(STEPS):
        arrivals = coupled_arrives if k else field_arrives
        rows = pl.ds(pl.multiple_of(c * units, units), units)
        for a in (1, 0, 2):
            if a == 1:
                centre_sources(arrivals)
            if a == 0:
                if k == 0:
                    loads[1].wait()
                totals = [convolve(k, 1, q) + wide(bias1[k])[:, :half] for q in range(2)]
                side_sources(arrivals)
            if k == 0:
                plane = whole[a]
            else:
                got = [cgot[a, s].astype(F32) for s in range(n_chan)]
                got = [jnp.concatenate([g[:share], g[share:]], axis=1) for g in got]
                plane = jnp.concatenate([fronts[a]] + got, axis=0).astype(BF16)
            if a == 1:
                permuted = jnp.dot(perm[k], plane, preferred_element_type=F32)
                back[...] = permuted
                front = permuted[:HALF]
            else:
                front = jnp.dot(perm[k, 0:HALF, :], plane, preferred_element_type=F32)
            if k == 0:
                fronts[a] = front
            for e in range(3):
                xpad[e, a * HALF : (a + 1) * HALF, PAD : PAD + NXY] = keep(front, e).astype(BF16)
            for b in range(3):
                for e in range(3):
                    at = ((a * 3 + b) * 3 + e) * HALF
                    patches[at : at + HALF, :] = xpad[e, a * HALF : (a + 1) * HALF, shifted(b, e)]
        for q in range(2):
            one = totals[q] + convolve(k, 0, q) + convolve(k, 2, q)
            hidden[k, q, rows, :] = jnp.maximum(one, 0.0).astype(BF16)
            for j in (2, 1):
                hidden_copy(k, q, j, c).start()
        if k == 0:
            for load in loads[2:]:
                load.wait()
        sums = []
        for q in range(2):
            summed = jnp.dot(wm[k, :, rows], hidden[k, q, rows, :], preferred_element_type=F32)
            for j in (1, 2, 3):
                theirs = pl.ds(pl.multiple_of(source(j) * units, units), units)
                here = hidden.at[k, q, theirs, :]
                arrive(1 + k, q, j, here)
                if j == 2:
                    hidden_copy(k, q, 3, source(2)).start()
                summed += jnp.dot(wm[k, :, theirs], here[...], preferred_element_type=F32)
            sums.append(summed)
        summed = jnp.concatenate(sums, axis=1)
        two = jnp.maximum(summed + wide(bias2[k]), 0.0)
        for e in range(3):
            hpad[e, :, PAD : PAD + NXY] = keep(two, e).astype(BF16)
        for b in range(3):
            for e in range(3):
                at = (b * 3 + e) * units
                patches3[at : at + units, :] = hpad[e, :, shifted(b, e)]
        weights = jnp.concatenate([wl[k, i] for i in range(9)], axis=1)
        parts = jnp.dot(weights, patches3[...], preferred_element_type=F32)
        for s in range(n_chan):
            for a in range(3):
                low = a * C + s * share
                psend[k, s, a] = jnp.concatenate(
                    [parts[low : low + share], parts[low + HALF : low + HALF + share]], axis=0
                ).astype(BF16)

        def send_parts(dz, j):
            to = place_of[j]
            copy(3 + k, dz, j, psend.at[k, to, 1 - dz], precv.at[k, 1 - dz, c]).start()

        each_peer(send_parts)
        precv[k, 1, c] = psend[k, c, 1]

        def parts_arrive(a, j):
            arrive(3 + k, a, j, precv.at[k, a, source(j)])

        centre_sources(parts_arrive)
        side_sources(parts_arrive)
        net = precv[k, 1, 0].astype(F32)
        for a in (1, 0, 2):
            for s in range(n_chan):
                if (a, s) != (1, 0):
                    net = net + precv[k, a, s].astype(F32)
        scales = pl.ds(pl.multiple_of(c * share, share), share)
        shifts = pl.ds(pl.multiple_of(HALF + c * share, share), share)
        arg = net[:share] + wide(bias3[k, scales, :]) + 2.0
        coupled = (back[shifts, :] + net[share:] + wide(bias3[k, shifts, :])) * jax.nn.sigmoid(arg)
        if k == 0:
            packed = jnp.concatenate([coupled[:, : NXY // 2], coupled[:, NXY // 2 :]], axis=0)
            csend[...] = packed.astype(BF16)

            def send_coupled(dz, j):
                copy(5, dz, j, csend, cgot.at[1 - dz, c]).start()

            each_peer(send_coupled)
            cgot[1, c] = packed.astype(BF16)
        else:
            final_send[...] = coupled
            keeper = n_chan // 2 + c // 2
            place = pl.ds(pl.multiple_of(lax.rem(c, 2) * share, share), share)
            last = pltpu.make_async_remote_copy(
                src_ref=final_send,
                dst_ref=final.at[place, :],
                send_sem=send_sem.at[6, 1, 0],
                recv_sem=recv_sem.at[6, 1, lax.rem(c, 2)],
                device_id={"chan": keeper},
                device_id_type=MESH,
            )

            @pl.when(keeper != c)
            def _():
                last.start()

            @pl.when(keeper == c)
            def _():
                final[place, :] = coupled

        soft = jnp.minimum(arg, 0.0) - jnp.log1p(jnp.exp(-jnp.abs(arg)))
        means = jnp.broadcast_to(jnp.sum(soft, axis=1, keepdims=True) * (1.0 / NXY), (share, share))
        diagonal = lax.broadcasted_iota(jnp.int32, (share, share), 0) == lax.broadcasted_iota(
            jnp.int32, (share, share), 1
        )
        logscale[k] = jnp.sum(jnp.where(diagonal, means, 0.0), axis=0, keepdims=True)

    for i in range(2):
        sender = 2 * (c - n_chan // 2) + i
        place = slice(i * share, (i + 1) * share)

        @pl.when(jnp.logical_and(c >= n_chan // 2, sender != c))
        def _():
            pltpu.make_async_remote_copy(
                src_ref=final_send,
                dst_ref=final.at[place, :],
                send_sem=send_sem.at[6, 1, 0],
                recv_sem=recv_sem.at[6, 1, i],
                device_id=peer(0, 1),
                device_id_type=MESH,
            ).wait_recv()

    @pl.when(c < n_chan // 2)
    def _():
        at = pl.ds(pl.multiple_of(lax.rem(c, 2) * own, own), own)
        final[...] = back[at, :]

    out = pltpu.make_async_copy(final, flowed.at[:, 0, :], out_sem)
    out.start()

    each_peer(lambda dz, j: copy(0, dz, j, whole.at[1, mine, :], whole.at[1 - dz, mine, :]).wait_send())
    for k in range(STEPS):
        for q in range(2):
            for j in (1, 2, 3):
                hidden_copy(k, q, j, source(2) if j == 3 else c).wait_send()
        each_peer(
            lambda dz, j: copy(
                3 + k, dz, j, psend.at[k, place_of[j], 1 - dz], precv.at[k, 1 - dz, c]
            ).wait_send()
        )
    each_peer(lambda dz, j: copy(5, dz, j, csend, cgot.at[1 - dz, c]).wait_send())

    @pl.when(n_chan // 2 + c // 2 != c)
    def _():
        last.wait_send()

    out.wait()


def local(field, order, w_first, b_first, w_middle, b_middle, w_last, b_last):
    n_chan = lax.axis_size("chan")
    share = HALF // n_chan
    own = C // n_chan
    units = w_first.shape[1]
    vmem = pl.BlockSpec(memory_space=pltpu.VMEM)
    hbm = pl.BlockSpec(memory_space=pl.ANY)
    flowed, logscale = pl.pallas_call(
        kernel,
        out_shape=(
            jax.ShapeDtypeStruct(field.shape, F32),
            jax.ShapeDtypeStruct((STEPS, 1, share), F32),
        ),
        in_specs=[hbm, vmem, hbm, vmem, hbm, vmem, hbm, vmem],
        out_specs=(hbm, vmem),
        scratch_shapes=[
            pltpu.VMEM((own, NXY), F32),
            pltpu.VMEM((STEPS, 27 * HALF, units), BF16),
            pltpu.VMEM(w_middle.shape, BF16),
            pltpu.VMEM((STEPS, 9, 3 * C, units), BF16),
            pltpu.VMEM((STEPS, units, 128), F32),
            pltpu.VMEM((STEPS, units, 128), F32),
            pltpu.VMEM((STEPS, C, 128), F32),
            pltpu.VMEM((STEPS, C, C), BF16),
            pltpu.VMEM((3, C, NXY), BF16),
            pltpu.VMEM((3, 3 * HALF, NXY + 2 * PAD), BF16),
            pltpu.VMEM((27 * HALF, NXY), BF16),
            pltpu.VMEM((STEPS, 2, n_chan * units, NXY // 2), BF16),
            pltpu.VMEM((3, units, NXY + 2 * PAD), BF16),
            pltpu.VMEM((9 * units, NXY), BF16),
            pltpu.VMEM((STEPS, n_chan, 3, 2 * share, NXY), BF16),
            pltpu.VMEM((STEPS, 3, n_chan, 2 * share, NXY), BF16),
            pltpu.VMEM((C, NXY), F32),
            pltpu.VMEM((2 * share, NXY // 2), BF16),
            pltpu.VMEM((3, n_chan, 2 * share, NXY // 2), BF16),
            pltpu.VMEM((3, HALF, NXY), F32),
            pltpu.VMEM((share, NXY), F32),
            pltpu.VMEM((own, NXY), F32),
            pltpu.SemaphoreType.DMA((9,)),
            pltpu.SemaphoreType.DMA((7, 3, n_chan)),
            pltpu.SemaphoreType.DMA((7, 3, n_chan)),
            pltpu.SemaphoreType.DMA,
        ],
        compiler_params=pltpu.CompilerParams(
            collective_id=0, has_side_effects=True, vmem_limit_bytes=62 << 20
        ),
    )(
        field, order, jnp.swapaxes(w_first, 1, 2), b_first, w_middle, b_middle,
        w_last.reshape(STEPS, 3, 9, C, units), b_last,
    )
    return flowed, jnp.swapaxes(logscale, 1, 2)


def solution(mesh):
    return jax.shard_map(
        local,
        mesh=mesh,
        in_specs=(
            P("chan", ("groups", "slab"), None),
            P(),
            P(None, "chan", None),
            P(None, "chan"),
            P(None, "chan", None),
            P(None, "chan"),
            P(None, None, "chan"),
            P(),
        ),
        out_specs=(P("chan", ("groups", "slab"), None), P(None, "chan", ("groups", "slab"))),
        check_vma=False,
    )
```

```python
import jax
import jax.numpy as jnp
from jax import lax
from jax.experimental import pallas as pl
from jax.experimental.pallas import tpu as pltpu
from jax.sharding import PartitionSpec as P

C = 64
HALF = 32
STEPS = 2
NY = 64
NXY = 512
PAD = 128
MESH = pl.DeviceIdType.MESH
F32 = jnp.float32
BF16 = jnp.bfloat16


def kernel(
    field, order, w_first, b_first, w_middle, b_middle, w_last, b_last,
    flowed, logscale,
    field_in, wf, wm, wl, bias1, bias2, bias3, perm,
    whole, xpad, patches, hidden, hpad, patches3, psend, precv,
    back, csend, cgot, fronts, final_send, final,
    load_sem, send_sem, recv_sem, out_sem,
):
    n_chan = lax.axis_size("chan")
    assert n_chan == 4
    n_slab = lax.axis_size("slab")
    c = lax.axis_index("chan")
    z = lax.axis_index("slab")
    share = HALF // n_chan
    own = C // n_chan
    units = wf.shape[2]
    has = {0: z > 0, 1: None, 2: z < n_slab - 1}

    place_of = (c, c + 1 - 2 * lax.rem(c, 2), lax.rem(c + 2, 4), 3 - c)

    def peer(dz, j):
        return {"slab": z + dz, "chan": place_of[j]}

    def each_peer(fn):
        for j in (2, 3, 1):
            fn(0, j)

        @pl.when(z > 0)
        def _():
            for j in range(n_chan):
                fn(-1, j)

        @pl.when(z < n_slab - 1)
        def _():
            for j in range(n_chan):
                fn(1, j)

    loads = [pltpu.make_async_copy(field.at[:, 0, :], field_in, load_sem.at[0])]
    loads.append(pltpu.make_async_copy(w_first, wf, load_sem.at[1]))
    loads.append(pltpu.make_async_copy(w_middle, wm, load_sem.at[2]))
    n = 3
    for k in range(STEPS):
        for a in range(3):
            loads.append(
                pltpu.make_async_copy(
                    w_last.at[k, a], wl.at[k, :, pl.ds(a * C, C), :], load_sem.at[n]
                )
            )
            n += 1
    for load in loads:
        load.start()

    barrier = pltpu.get_barrier_semaphore()

    def greet(dz, j):
        pl.semaphore_signal(barrier, inc=1, device_id=peer(dz, j), device_id_type=MESH)

    each_peer(greet)

    for k in range(STEPS):
        row = order[k : k + 1, :]
        hit = (lax.broadcasted_iota(jnp.int32, (C, C), 0) == row).astype(F32)
        perm[k] = hit.T.astype(BF16)
        bias1[k] = jnp.broadcast_to(b_first[k : k + 1, :].astype(F32), (128, units)).T
        bias2[k] = jnp.broadcast_to(b_middle[k : k + 1, :].astype(F32), (128, units)).T
        bias3[k] = jnp.broadcast_to(b_last[k : k + 1, :].astype(F32), (128, C)).T
    for e in range(3):
        xpad[e, :, 0:PAD] = jnp.zeros((3 * HALF, PAD), BF16)
        xpad[e, :, PAD + NXY :] = jnp.zeros((3 * HALF, PAD), BF16)
        hpad[e, :, 0:PAD] = jnp.zeros((units, PAD), BF16)
        hpad[e, :, PAD + NXY :] = jnp.zeros((units, PAD), BF16)
    for a in (0, 2):

        @pl.when(jnp.logical_not(has[a]))
        def _():
            whole[a] = jnp.zeros((C, NXY), BF16)
            cgot[a] = jnp.zeros((n_chan, 2 * share, NXY // 2), BF16)
            for k in range(STEPS):
                precv[k, a] = jnp.zeros((n_chan, 2 * share, NXY), BF16)

    mine = pl.ds(pl.multiple_of(c * own, own), own)
    loads[0].wait()
    whole[1, mine, :] = field_in[...].astype(BF16)

    sides = jnp.where(z > 0, 1, 0) + jnp.where(z < n_slab - 1, 1, 0)
    pl.semaphore_wait(barrier, n_chan - 1 + n_chan * sides)

    def copy(phase, dz, j, src, dst):
        return pltpu.make_async_remote_copy(
            src_ref=src,
            dst_ref=dst,
            send_sem=send_sem.at[phase, 1 - dz, j],
            recv_sem=recv_sem.at[phase, 1 - dz, j],
            device_id=peer(dz, j),
            device_id_type=MESH,
        )

    def arrive(phase, a, j, dst):
        pltpu.make_async_remote_copy(
            src_ref=dst,
            dst_ref=dst,
            send_sem=send_sem.at[phase, a, j],
            recv_sem=recv_sem.at[phase, a, j],
            device_id=peer(0, 1),
            device_id_type=MESH,
        ).wait_recv()

    def centre_sources(fn):
        for j in (1, 2, 3):
            fn(1, j)

    def side_sources(fn):
        @pl.when(z > 0)
        def _():
            for j in range(n_chan):
                fn(0, j)

        @pl.when(z < n_slab - 1)
        def _():
            for j in range(n_chan):
                fn(2, j)

    def source(j):
        return place_of[j]

    def send_field(dz, j):
        copy(0, dz, j, whole.at[1, mine, :], whole.at[1 - dz, mine, :]).start()

    each_peer(send_field)

    def field_arrives(a, j):
        rows = pl.ds(pl.multiple_of(source(j) * own, own), own)
        arrive(0, a, j, whole.at[a, rows, :])

    y = lax.rem(lax.broadcasted_iota(jnp.int32, (1, NXY), 1), NY)

    def keep(values, e):
        if e == 0:
            return jnp.where(y == NY - 1, 0.0, values)
        if e == 2:
            return jnp.where(y == 0, 0.0, values)
        return values

    def shifted(b, e):
        start = PAD + NY * (b - 1) + (e - 1)
        return slice(start, start + NXY)

    def wide(column):
        return jnp.concatenate([column] * (NXY // 128), axis=1)

    def coupled_arrives(a, j):
        arrive(5, a, j, cgot.at[a, source(j)])

    half = NXY // 2

    def convolve(k, a, q):
        depth = slice(a * 9 * HALF, (a + 1) * 9 * HALF)
        return lax.dot_general(
            wf[k, depth, :],
            patches[depth, q * half : (q + 1) * half],
            (((0,), (0,)), ((), ())),
            preferred_element_type=F32,
        )

    def hidden_copy(k, q, j, owner):
        part = hidden.at[k, q, pl.ds(pl.multiple_of(owner * units, units), units), :]
        return pltpu.make_async_remote_copy(
            src_ref=part,
            dst_ref=part,
            send_sem=send_sem.at[1 + k, q, j],
            recv_sem=recv_sem.at[1 + k, q, j],
            device_id=peer(0, 1 if j == 3 else j),
            device_id_type=MESH,
        )

    for k in range(STEPS):
        arrivals = coupled_arrives if k else field_arrives
        rows = pl.ds(pl.multiple_of(c * units, units), units)
        for a in (1, 0, 2):
            if a == 1:
                centre_sources(arrivals)
            if a == 0:
                if k == 0:
                    loads[1].wait()
                totals = [convolve(k, 1, q) + wide(bias1[k])[:, :half] for q in range(2)]
                side_sources(arrivals)
            if k == 0:
                plane = whole[a]
            else:
                got = [cgot[a, s].astype(F32) for s in range(n_chan)]
                got = [jnp.concatenate([g[:share], g[share:]], axis=1) for g in got]
                plane = jnp.concatenate([fronts[a]] + got, axis=0).astype(BF16)
            if a == 1:
                permuted = jnp.dot(perm[k], plane, preferred_element_type=F32)
                back[...] = permuted
                front = permuted[:HALF]
            else:
                front = jnp.dot(perm[k, 0:HALF, :], plane, preferred_element_type=F32)
            if k == 0:
                fronts[a] = front
            for e in range(3):
                xpad[e, a * HALF : (a + 1) * HALF, PAD : PAD + NXY] = keep(front, e).astype(BF16)
            for b in range(3):
                for e in range(3):
                    at = ((a * 3 + b) * 3 + e) * HALF
                    patches[at : at + HALF, :] = xpad[e, a * HALF : (a + 1) * HALF, shifted(b, e)]
        for q in range(2):
            one = totals[q] + convolve(k, 0, q) + convolve(k, 2, q)
            hidden[k, q, rows, :] = jnp.maximum(one, 0.0).astype(BF16)
            for j in (2, 1):
                hidden_copy(k, q, j, c).start()
        if k == 0:
            for load in loads[2:]:
                load.wait()
        sums = []
        for q in range(2):
            summed = jnp.dot(wm[k, :, rows], hidden[k, q, rows, :], preferred_element_type=F32)
            sums.append(summed)
        for q, j in ((0, 1), (0, 2), (1, 1), (1, 2), (0, 3), (1, 3)):
            theirs = pl.ds(pl.multiple_of(source(j) * units, units), units)
            here = hidden.at[k, q, theirs, :]
            arrive(1 + k, q, j, here)
            if j == 2:
                hidden_copy(k, q, 3, source(2)).start()
            sums[q] += jnp.dot(wm[k, :, theirs], here[...], preferred_element_type=F32)
        summed = jnp.concatenate(sums, axis=1)
        two = jnp.maximum(summed + wide(bias2[k]), 0.0)
        for e in range(3):
            hpad[e, :, PAD : PAD + NXY] = keep(two, e).astype(BF16)
        for b in range(3):
            for e in range(3):
                at = (b * 3 + e) * units
                patches3[at : at + units, :] = hpad[e, :, shifted(b, e)]
        weights = jnp.concatenate([wl[k, i] for i in range(9)], axis=1)
        parts = jnp.dot(weights, patches3[...], preferred_element_type=F32)
        for s in range(n_chan):
            for a in range(3):
                low = a * C + s * share
                psend[k, s, a] = jnp.concatenate(
                    [parts[low : low + share], parts[low + HALF : low + HALF + share]], axis=0
                ).astype(BF16)

        def send_parts(dz, j):
            to = place_of[j]
            copy(3 + k, dz, j, psend.at[k, to, 1 - dz], precv.at[k, 1 - dz, c]).start()

        each_peer(send_parts)
        precv[k, 1, c] = psend[k, c, 1]

        def parts_arrive(a, j):
            arrive(3 + k, a, j, precv.at[k, a, source(j)])

        centre_sources(parts_arrive)
        side_sources(parts_arrive)
        net = precv[k, 1, 0].astype(F32)
        for a in (1, 0, 2):
            for s in range(n_chan):
                if (a, s) != (1, 0):
                    net = net + precv[k, a, s].astype(F32)
        scales = pl.ds(pl.multiple_of(c * share, share), share)
        shifts = pl.ds(pl.multiple_of(HALF + c * share, share), share)
        arg = net[:share] + wide(bias3[k, scales, :]) + 2.0
        coupled = (back[shifts, :] + net[share:] + wide(bias3[k, shifts, :])) * jax.nn.sigmoid(arg)
        if k == 0:
            packed = jnp.concatenate([coupled[:, : NXY // 2], coupled[:, NXY // 2 :]], axis=0)
            csend[...] = packed.astype(BF16)

            def send_coupled(dz, j):
                copy(5, dz, j, csend, cgot.at[1 - dz, c]).start()

            each_peer(send_coupled)
            cgot[1, c] = packed.astype(BF16)
        else:
            final_send[...] = coupled
            keeper = n_chan // 2 + c // 2
            place = pl.ds(pl.multiple_of(lax.rem(c, 2) * share, share), share)
            last = pltpu.make_async_remote_copy(
                src_ref=final_send,
                dst_ref=final.at[place, :],
                send_sem=send_sem.at[6, 1, 0],
                recv_sem=recv_sem.at[6, 1, lax.rem(c, 2)],
                device_id={"chan": keeper},
                device_id_type=MESH,
            )

            @pl.when(keeper != c)
            def _():
                last.start()

            @pl.when(keeper == c)
            def _():
                final[place, :] = coupled

        soft = jnp.minimum(arg, 0.0) - jnp.log1p(jnp.exp(-jnp.abs(arg)))
        means = jnp.broadcast_to(jnp.sum(soft, axis=1, keepdims=True) * (1.0 / NXY), (share, share))
        diagonal = lax.broadcasted_iota(jnp.int32, (share, share), 0) == lax.broadcasted_iota(
            jnp.int32, (share, share), 1
        )
        logscale[k] = jnp.sum(jnp.where(diagonal, means, 0.0), axis=0, keepdims=True)

    for i in range(2):
        sender = 2 * (c - n_chan // 2) + i
        place = slice(i * share, (i + 1) * share)

        @pl.when(jnp.logical_and(c >= n_chan // 2, sender != c))
        def _():
            pltpu.make_async_remote_copy(
                src_ref=final_send,
                dst_ref=final.at[place, :],
                send_sem=send_sem.at[6, 1, 0],
                recv_sem=recv_sem.at[6, 1, i],
                device_id=peer(0, 1),
                device_id_type=MESH,
            ).wait_recv()

    @pl.when(c < n_chan // 2)
    def _():
        at = pl.ds(pl.multiple_of(lax.rem(c, 2) * own, own), own)
        final[...] = back[at, :]

    out = pltpu.make_async_copy(final, flowed.at[:, 0, :], out_sem)
    out.start()

    each_peer(lambda dz, j: copy(0, dz, j, whole.at[1, mine, :], whole.at[1 - dz, mine, :]).wait_send())
    for k in range(STEPS):
        for q in range(2):
            for j in (1, 2, 3):
                hidden_copy(k, q, j, source(2) if j == 3 else c).wait_send()
        each_peer(
            lambda dz, j: copy(
                3 + k, dz, j, psend.at[k, place_of[j], 1 - dz], precv.at[k, 1 - dz, c]
            ).wait_send()
        )
    each_peer(lambda dz, j: copy(5, dz, j, csend, cgot.at[1 - dz, c]).wait_send())

    @pl.when(n_chan // 2 + c // 2 != c)
    def _():
        last.wait_send()

    out.wait()


def local(field, order, w_first, b_first, w_middle, b_middle, w_last, b_last):
    n_chan = lax.axis_size("chan")
    share = HALF // n_chan
    own = C // n_chan
    units = w_first.shape[1]
    vmem = pl.BlockSpec(memory_space=pltpu.VMEM)
    hbm = pl.BlockSpec(memory_space=pl.ANY)
    flowed, logscale = pl.pallas_call(
        kernel,
        out_shape=(
            jax.ShapeDtypeStruct(field.shape, F32),
            jax.ShapeDtypeStruct((STEPS, 1, share), F32),
        ),
        in_specs=[hbm, vmem, hbm, vmem, hbm, vmem, hbm, vmem],
        out_specs=(hbm, vmem),
        scratch_shapes=[
            pltpu.VMEM((own, NXY), F32),
            pltpu.VMEM((STEPS, 27 * HALF, units), BF16),
            pltpu.VMEM(w_middle.shape, BF16),
            pltpu.VMEM((STEPS, 9, 3 * C, units), BF16),
            pltpu.VMEM((STEPS, units, 128), F32),
            pltpu.VMEM((STEPS, units, 128), F32),
            pltpu.VMEM((STEPS, C, 128), F32),
            pltpu.VMEM((STEPS, C, C), BF16),
            pltpu.VMEM((3, C, NXY), BF16),
            pltpu.VMEM((3, 3 * HALF, NXY + 2 * PAD), BF16),
            pltpu.VMEM((27 * HALF, NXY), BF16),
            pltpu.VMEM((STEPS, 2, n_chan * units, NXY // 2), BF16),
            pltpu.VMEM((3, units, NXY + 2 * PAD), BF16),
            pltpu.VMEM((9 * units, NXY), BF16),
            pltpu.VMEM((STEPS, n_chan, 3, 2 * share, NXY), BF16),
            pltpu.VMEM((STEPS, 3, n_chan, 2 * share, NXY), BF16),
            pltpu.VMEM((C, NXY), F32),
            pltpu.VMEM((2 * share, NXY // 2), BF16),
            pltpu.VMEM((3, n_chan, 2 * share, NXY // 2), BF16),
            pltpu.VMEM((3, HALF, NXY), F32),
            pltpu.VMEM((share, NXY), F32),
            pltpu.VMEM((own, NXY), F32),
            pltpu.SemaphoreType.DMA((9,)),
            pltpu.SemaphoreType.DMA((7, 3, n_chan)),
            pltpu.SemaphoreType.DMA((7, 3, n_chan)),
            pltpu.SemaphoreType.DMA,
        ],
        compiler_params=pltpu.CompilerParams(
            collective_id=0, has_side_effects=True, vmem_limit_bytes=62 << 20
        ),
    )(
        field, order, jnp.swapaxes(w_first, 1, 2), b_first, w_middle, b_middle,
        w_last.reshape(STEPS, 3, 9, C, units), b_last,
    )
    return flowed, jnp.swapaxes(logscale, 1, 2)


def solution(mesh):
    return jax.shard_map(
        local,
        mesh=mesh,
        in_specs=(
            P("chan", ("groups", "slab"), None),
            P(),
            P(None, "chan", None),
            P(None, "chan"),
            P(None, "chan", None),
            P(None, "chan"),
            P(None, None, "chan"),
            P(),
        ),
        out_specs=(P("chan", ("groups", "slab"), None), P(None, "chan", ("groups", "slab"))),
        check_vma=False,
    )
```
